32 devices in a mesh: grp: 2 (over y), dev: 16 (over z, x, core).
Axes of the slice: x: 2, y: 2, z: 4, core: 2. Of those that a mesh axis runs over, the one named last changes fastest.
Arguments:
- spectra: bfloat16 [512, 2, 2048], P(('grp', 'dev')), may hold values from -6 to 6
- stack_in: bfloat16 [2, 256, 512, 128], P(None, None, ('grp', 'dev')), may hold values from -6 to 6
- plan: int32 [2], replicated, may hold values from 0 to 1
- seg_lengths: int32 [16], replicated, may hold values from 1 to 64, 512 in all
- taps: float32 [9], replicated, may hold values from -3 to 3
Outputs:
- stack: float32 [2, 256, 512, 128], P(None, None, ('grp', 'dev'))
- filtered: float32 [2, 256, 512, 128], P(None, None, ('grp', 'dev'))
The draws below stay inside these ranges and needn't reach their ends.
All inputs are finite; a program needn't handle non-finite values.
Results may differ from the reference program's by a relative error of at most 0.0026.
Values may be sent and summed in bfloat16 or wider, within the bound.
No kernel may reach another device: no remote copies, remote signals or barrier semaphores. Data moves between devices by JAX's collectives and lax.ppermute only.
A program may use at most 64 MiB of HBM per device.

```python
import math
import jax
import jax.numpy as jnp
import numpy as np
from jax import lax

F = 2048
SRC = 256
LAGS = 128
HALF = 4
STEPS = 2
NSEG = 16
CHANNELS = 512
NBLK = 2


def shard_levels(rng, dims, shards, least, largest):
    factor_of = 1.0
    for dim, shards_of in shards:
        steps = jax.random.uniform(jax.random.fold_in(jax.random.fold_in(rng, 6), dim), (shards_of,), jnp.float32, least / len(shards), largest / len(shards))
        factor_of = factor_of * jnp.repeat(jnp.exp(steps), dims[dim] // shards_of).reshape((-1,) + (1,) * (len(dims) - 1 - dim))
    return factor_of


def profile(number_of, total, most, lean):
    portions = [(1 << 20) // math.isqrt(grade ** lean) + 1 for grade in range(2, number_of + 1)]
    spare, holding = total - most - (number_of - 1), [1] * (number_of - 1)
    while spare > 0:
        movable = [i for i in range(number_of - 1) if holding[i] < most]
        whole, remaining = sum([portions[i] for i in movable]), spare
        for i in movable:
            extra = min(most - holding[i], max(1, remaining * portions[i] // whole), spare)
            holding[i] = holding[i] + extra
            spare = spare - extra
    return np.array([most] + holding)


def uneven_parts(stream_key, number_of, total, reach, skew):
    if number_of == 2:
        one = jax.random.randint(stream_key, (), max(1, total - reach), min(reach, total - 1) + 1)
        return jnp.stack([one, total - one])
    lengths = jnp.asarray(profile(number_of, total, reach, skew), jnp.int32)
    twos = (number_of - 1) // 2
    donor, receiver = lengths[1:1 + 2 * twos:2], lengths[2:2 + 2 * twos:2]
    room = jnp.minimum(donor - 1, reach - receiver)
    passed = jax.random.randint(jax.random.fold_in(stream_key, 1), (twos,), 0, 1 << 20) % (room + 1)
    lengths = lengths.at[1:1 + 2 * twos:2].set(donor - passed).at[2:2 + 2 * twos:2].set(receiver + passed)
    return lengths[jax.random.permutation(jax.random.fold_in(stream_key, 2), number_of)]


def bell_draw(key, dims, scale, most, split=(), held_as=jnp.bfloat16):
    level = shard_levels(key, dims, split, -0.22, 0.18) if split else 1.0
    entries = jax.random.normal(key, dims, jnp.float32) * scale * level
    return jnp.minimum(jnp.maximum(entries, -most), most).astype(held_as)


def setup_inputs(seed: int = 0) -> dict:
    splits = jax.random.split(jax.random.key(seed), 6)
    return {
        "spectra": bell_draw(splits[0], (CHANNELS, 2, F), 1.0, 6.0, ((0, 32),)),
        "stack_in": bell_draw(splits[1], (STEPS, SRC, CHANNELS, LAGS), 1.0, 6.0, ((2, 32),)),
        "plan": jax.random.randint(splits[2], (STEPS,), 0, NBLK).astype(jnp.int32),
        "seg_lengths": uneven_parts(splits[3], NSEG, CHANNELS, CHANNELS // 8, 2).astype(jnp.int32),
        "taps": bell_draw(splits[4], (2 * HALF + 1,), 0.5, 3.0, (), jnp.float32),
    }


def whiten(spectra):
    real_part = spectra[:, 0, :].astype(jnp.float32)
    imag_part = spectra[:, 1, :].astype(jnp.float32)
    magnitude = jnp.sqrt(real_part * real_part + imag_part * imag_part)
    factor = 1.0 / jnp.maximum(magnitude, 0.25)
    return jnp.stack([real_part * factor, imag_part * factor], axis=1).astype(jnp.bfloat16)

def make_table(freqs, lags):
    bins = jnp.arange(freqs, dtype=jnp.int32)[:, None]
    shifts = jnp.arange(lags, dtype=jnp.int32)[None, :] - lags // 2
    modulus = bins * shifts % (2 * freqs)
    angle = modulus.astype(jnp.float32) * (math.pi / freqs)
    scale_value = 1.0 / math.sqrt(freqs)
    table = jnp.concatenate([jnp.cos(angle), -jnp.sin(angle)], axis=0) * scale_value
    return table.astype(jnp.bfloat16)

def cross_block(sources, receivers, table):
    src_re = sources[:, 0, :].astype(jnp.float32)[:, None, :]
    src_im = sources[:, 1, :].astype(jnp.float32)[:, None, :]
    rec_re = receivers[:, 0, :].astype(jnp.float32)[None, :, :]
    rec_im = receivers[:, 1, :].astype(jnp.float32)[None, :, :]
    cross_re = src_re * rec_re + src_im * rec_im
    cross_im = src_im * rec_re - src_re * rec_im
    cross = jnp.concatenate([cross_re, cross_im], axis=-1).astype(jnp.bfloat16)
    rows = sources.shape[0] * receivers.shape[0]
    flat = cross.reshape(rows, cross.shape[-1])
    result = jnp.dot(flat, table, preferred_element_type=jnp.float32)
    return result.reshape(sources.shape[0], receivers.shape[0], table.shape[1])

def segment_of(channel_ids, seg_lengths):
    bounds = jnp.cumsum(seg_lengths)[:-1]
    return lax.optimization_barrier(jnp.sum((channel_ids[:, None] >= bounds[None, :]).astype(jnp.int32), axis=1))

def mixing_weights(seg_ids, taps, count):
    width = (taps.shape[0] - 1) // 2
    centre = seg_ids[width:width + count]
    columns = []
    for offset in range(taps.shape[0]):
        same = (seg_ids[offset:offset + count] == centre).astype(jnp.float32)
        columns.append(taps[offset] * same)
    return jnp.stack(columns, axis=1)

def apply_filter(extended, mixing, dim, count):
    total = jnp.zeros(extended.shape[:dim] + (count,) + extended.shape[dim + 1:], jnp.float32)
    for offset in range(mixing.shape[1]):
        part = lax.slice_in_dim(extended, offset, offset + count, axis=dim)
        shape = [1] * extended.ndim
        shape[dim] = count
        total = total + mixing[:, offset].reshape(shape) * part
    return total

def reference(spectra, stack_in, plan, seg_lengths, taps):
    white = whiten(spectra)
    table = make_table(F, LAGS)
    stacks = []
    for step in range(STEPS):
        first = (plan[step] * SRC).astype(jnp.int32)
        sources = lax.dynamic_slice_in_dim(white, first, SRC, 0)
        grouped = sources.reshape(SRC // 4, 4, 2, F)
        corr = lax.map(lambda block: cross_block(block, white, table), grouped)
        corr = corr.reshape(SRC, CHANNELS, LAGS)
        stacks.append(stack_in[step].astype(jnp.float32) + corr)
    stack = jnp.stack(stacks, axis=0)
    channel_ids = jnp.arange(CHANNELS + 2 * HALF, dtype=jnp.int32) - HALF
    seg_ids = segment_of(channel_ids, seg_lengths)
    mixing = mixing_weights(seg_ids, taps, CHANNELS)
    padded = jnp.pad(stack, ((0, 0), (0, 0), (HALF, HALF), (0, 0)))
    filtered = apply_filter(padded, mixing, 2, CHANNELS)
    return (stack, filtered)
```

```python
import functools
import math

import jax
import jax.numpy as jnp
import ml_dtypes
import numpy as np
from jax import lax
from jax.experimental import pallas as pl
from jax.experimental.pallas import tpu as pltpu
from jax.sharding import PartitionSpec as P

AXES = ("grp", "dev")
FILL = 512


def whiten(spectra):
    real_part = spectra[:, 0, :].astype(jnp.float32)
    imag_part = spectra[:, 1, :].astype(jnp.float32)
    magnitude = jnp.sqrt(real_part * real_part + imag_part * imag_part)
    factor = 1.0 / jnp.maximum(magnitude, 0.25)
    pair = jnp.concatenate([real_part * factor, imag_part * factor], axis=1)
    return pair.astype(jnp.bfloat16)


def make_table(freqs, lags):
    bins = np.arange(freqs, dtype=np.int64)[None, :]
    shifts = np.arange(lags, dtype=np.int64)[:, None] - lags // 2
    modulus = (bins * shifts) % (2 * freqs)
    angle = modulus.astype(np.float64) * (math.pi / freqs)
    table = np.concatenate([np.cos(angle), -np.sin(angle)], axis=1) / math.sqrt(freqs)
    return jnp.asarray(table.astype(np.float32).astype(ml_dtypes.bfloat16))


def segment_of(channel_ids, seg_lengths):
    bounds = jnp.cumsum(seg_lengths)[:-1]
    return jnp.sum((channel_ids[:, None] >= bounds[None, :]).astype(jnp.int32), axis=1)


def mixing_weights(seg_ids, taps, count):
    width = (taps.shape[0] - 1) // 2
    centre = seg_ids[width : width + count]
    columns = []
    for offset in range(taps.shape[0]):
        same = (seg_ids[offset : offset + count] == centre).astype(jnp.float32)
        columns.append(taps[offset] * same)
    return jnp.stack(columns, axis=0)


def weights_kernel(receivers, table, weights):
    count, lags, freqs = receivers.shape[0], table.shape[0], table.shape[1] // 2
    fill = min(FILL, freqs)

    def body(step, _):
        first = pl.multiple_of(step * fill, fill)
        low, high = pl.ds(first, fill), pl.ds(freqs + first, fill)
        cosine = table[:, low].astype(jnp.float32)
        sine = table[:, high].astype(jnp.float32)
        for c in range(count):
            real_part = receivers[pl.ds(c, 1), low].astype(jnp.float32)
            imag_part = receivers[pl.ds(c, 1), high].astype(jnp.float32)
            rows = pl.ds(c * lags, lags)
            weights[rows, low] = (real_part * cosine - imag_part * sine).astype(jnp.bfloat16)
            weights[rows, high] = (imag_part * cosine + real_part * sine).astype(jnp.bfloat16)
        return 0

    lax.fori_loop(0, freqs // fill, body, 0)


def make_weights(receivers, table):
    count, bins = receivers.shape
    lags = table.shape[0]
    return pl.pallas_call(
        weights_kernel,
        out_shape=pltpu.VMEM((count * lags, bins), jnp.bfloat16),
        in_specs=[pl.BlockSpec(memory_space=pltpu.VMEM)] * 2,
        out_specs=pl.BlockSpec(memory_space=pltpu.VMEM),
        compiler_params=pltpu.CompilerParams(vmem_limit_bytes=8 << 20),
        cost_estimate=pl.CostEstimate(
            flops=3 * count * lags * bins, bytes_accessed=2 * count * lags * bins, transcendentals=0
        ),
        name="make_weights",
    )(receivers, table)


def block_kernel(unit, parts, info, mix, *refs):
    sources = refs[:parts]
    weights, kept = refs[parts], refs[parts + 1]
    stack_out, filtered_out = refs[-7], refs[-6]
    lhs, corr, stack_buf, filtered_buf, sems = refs[-5:]
    rows = lhs.shape[0]
    units = rows // unit
    steps, _, reach, lags = kept.shape
    taps, shard, _ = mix.shape
    width = (taps - 1) // 2
    first = 0
    for part in sources:
        lhs[pl.ds(first, part.shape[0]), :] = part[...]
        first += part.shape[0]
    group = 4
    columns = group * lags

    def product(step, _):
        at = pl.multiple_of(step * columns, columns)
        out = lax.dot_general(
            lhs[...],
            weights[pl.ds(at, columns), :],
            (((1,), (1,)), ((), ())),
            preferred_element_type=jnp.float32,
        )
        for j in range(group):
            channel = step * group + j
            corr[pl.ds(channel, rows, stride=reach), :] = out[:, j * lags : (j + 1) * lags]
        return 0

    lax.fori_loop(0, reach // group, product, 0)

    def copies(slot, step, row):
        return (
            pltpu.make_async_copy(
                stack_buf.at[slot], stack_out.at[step, pl.ds(row, unit)], sems.at[0, slot]
            ),
            pltpu.make_async_copy(
                filtered_buf.at[slot], filtered_out.at[step, pl.ds(row, unit)], sems.at[1, slot]
            ),
        )

    def finish(slot):
        for copy in copies(slot, 0, 0):
            copy.wait()

    def visit(number, used):
        u, step = number // steps, number % steps
        row = info[steps + units + u]

        def work(used):
            slot = used % 2

            @pl.when(used >= 2)
            def _():
                finish(slot)

            for i in range(unit):
                at = pl.multiple_of((u * unit + i) * reach, reach)
                whole = corr[pl.ds(at, reach), :] + kept[step, row + i].astype(jnp.float32)
                stack_buf[slot, i] = whole[:shard]
                total = mix[width] * whole[:shard]
                for offset in range(-width, width + 1):
                    if offset:
                        moved = pltpu.roll(whole, (-offset) % reach, 0)[:shard]
                        total = total + mix[width + offset] * moved
                filtered_buf[slot, i] = total
            for copy in copies(slot, step, row):
                copy.start()
            return used + 1

        return lax.cond(info[step] == info[steps + u], work, lambda used: used, used)

    used = lax.fori_loop(0, units * steps, visit, 0)

    @pl.when(used >= 1)
    def _():
        finish((used - 1) % 2)

    @pl.when(used >= 2)
    def _():
        finish(used % 2)


def block(sources, weights, kept, mix, info, unit, outs, out_shape):
    rows = sum(part.shape[0] for part in sources)
    steps, count, reach, lags = kept.shape
    taps, shard, _ = mix.shape
    bins = weights.shape[1]
    vmem, anywhere = pl.BlockSpec(memory_space=pltpu.VMEM), pl.BlockSpec(memory_space=pl.ANY)
    carried = list(outs)
    before = 2 + len(sources) + 2
    return pl.pallas_call(
        functools.partial(block_kernel, unit, len(sources)),
        out_shape=(out_shape, out_shape),
        in_specs=[pl.BlockSpec(memory_space=pltpu.SMEM)]
        + [vmem] * (1 + len(sources) + 2)
        + [anywhere] * len(carried),
        out_specs=(anywhere, anywhere),
        scratch_shapes=[
            pltpu.VMEM((rows, bins), jnp.bfloat16),
            pltpu.VMEM((rows * reach, lags), jnp.float32),
            pltpu.VMEM((2, unit, shard, lags), jnp.float32),
            pltpu.VMEM((2, unit, shard, lags), jnp.float32),
            pltpu.SemaphoreType.DMA((2, 2)),
        ],
        input_output_aliases={before: 0, before + 1: 1} if carried else {},
        compiler_params=pltpu.CompilerParams(vmem_limit_bytes=14 << 20),
        cost_estimate=pl.CostEstimate(
            flops=2 * rows * bins * reach * lags,
            bytes_accessed=8 * rows * shard * lags,
            transcendentals=0,
        ),
        name="block",
    )(info, mix, *sources, weights, kept, *carried)


def pairs(groups, devs, move):
    lines = devs // 4
    listed = []
    for g in range(groups):
        for line in range(lines):
            for side in range(2):
                for core in range(2):
                    h, other, flank, die = move(g, line, side, core)
                    listed.append(
                        (
                            g * devs + (line * 2 + side) * 2 + core,
                            h * devs + (other * 2 + flank) * 2 + die,
                        )
                    )
    return listed


def gather_small(own):
    groups, devs = lax.axis_size("grp"), lax.axis_size("dev")
    lines = devs // 4
    g, d = lax.axis_index("grp"), lax.axis_index("dev")
    line, side, core = d // 4, (d // 2) % 2, d % 2

    def send(value, move):
        return lax.ppermute(value, AXES, pairs(groups, devs, move))

    held = [own]
    for k in range(1, lines):
        held.append(send(own, lambda h, n, s, c: (h, (n + k) % lines, s, c)))
    first = jnp.concatenate(held, axis=0)
    second = send(first, lambda h, n, s, c: (h, n, 1 - s, c) if c == 0 else (1 - h, n, s, c))
    near = jnp.concatenate([first, second], axis=0)
    far = send(near, lambda h, n, s, c: (h, n, 1 - s, c) if c == 1 else (1 - h, n, s, c))
    near_other = send(near, lambda h, n, s, c: (h, n, s, 1 - c))
    far_other = send(far, lambda h, n, s, c: (h, n, s, 1 - c))

    def owners(core, far):
        listed = []
        for j in range(2):
            flip_side = jnp.where(core == 0, j, far)
            flip_group = jnp.where(core == 0, far, j)
            for k in range(lines):
                at_group = jnp.bitwise_xor(g, flip_group)
                at_side = jnp.bitwise_xor(side, flip_side)
                at_line = (line - k + lines) % lines
                listed.append(at_group * devs + (at_line * 2 + at_side) * 2 + core)
        return listed

    return (
        ((near, near_other), jnp.stack(owners(core, 0) + owners(1 - core, 0))),
        ((far, far_other), jnp.stack(owners(core, 1) + owners(1 - core, 1))),
    )


def shards(spectra, stack_in, plan, seg_lengths, taps):
    shard, _, freqs = spectra.shape
    steps, source_count, _, lags = stack_in.shape
    width = (taps.shape[0] - 1) // 2
    groups, devs = lax.axis_size("grp"), lax.axis_size("dev")
    total = groups * devs
    group_channels = devs * shard
    reach = shard + 2 * width

    own = whiten(spectra)
    start_channel = lax.axis_index(AXES) * shard
    channel_ids = start_channel + jnp.arange(reach, dtype=jnp.int32) - width
    mixing = mixing_weights(segment_of(channel_ids, seg_lengths), taps, shard)
    mix = jnp.broadcast_to(mixing[:, :, None], mixing.shape + (lags,))

    edge = steps * source_count * width

    def packed(first):
        stacks = lax.slice_in_dim(stack_in, first, first + width, axis=2)
        raw = lax.slice_in_dim(spectra, first, first + width, axis=0)
        return jnp.concatenate([stacks.reshape(edge, lags), raw.reshape(-1, lags)], axis=0)

    low = lax.ppermute(packed(shard - width), AXES, [(i, i + 1) for i in range(total - 1)])
    high = lax.ppermute(packed(0), AXES, [(i + 1, i) for i in range(total - 1)])

    def stacks_of(edges):
        return edges[:edge].reshape(steps, source_count, width, lags)

    def white_of(edges):
        return whiten(edges[edge:].reshape(width, 2, freqs))

    kept = jnp.concatenate([stack_in, stacks_of(high), stacks_of(low)], axis=2)
    receivers = jnp.concatenate([own, white_of(high), white_of(low)], axis=0)
    weights = make_weights(receivers, make_table(freqs, lags))

    out_shape = jax.ShapeDtypeStruct((steps, source_count, shard, lags), jnp.float32)
    outs = ()
    if groups == 2 and devs % 4 == 0 and total * shard == 2 * source_count:
        for sources, owners in gather_small(own):
            channels = owners * shard
            info = jnp.concatenate([plan, channels // source_count, channels % source_count])
            outs = block(
                sources, weights, kept, mix, info.astype(jnp.int32), shard, outs, out_shape
            )
        return outs
    for step in range(steps):
        first = plan[step] * source_count
        mine = jnp.where(lax.axis_index("grp") == first // group_channels, own, 0)
        piece = lax.psum(mine.astype(own.dtype), "grp")
        whole = lax.all_gather(piece, "dev", axis=0, tiled=True)
        sources = lax.dynamic_slice_in_dim(whole, first % group_channels, source_count, 0)
        units = source_count // shard
        info = jnp.concatenate(
            [
                jnp.arange(steps, dtype=jnp.int32),
                jnp.full((units,), step, jnp.int32),
                jnp.arange(units, dtype=jnp.int32) * shard,
            ]
        )
        outs = block((sources,), weights, kept, mix, info, shard, outs, out_shape)
    return outs


def solution(mesh):
    placed = (P(AXES, None, None), P(None, None, AXES, None), P(), P(), P())
    return jax.shard_map(
        shards,
        mesh=mesh,
        in_specs=placed,
        out_specs=(P(None, None, AXES, None), P(None, None, AXES, None)),
        check_vma=False,
    )
```

```python
import functools
import math

import jax
import jax.numpy as jnp
import ml_dtypes
import numpy as np
from jax import lax
from jax.experimental import pallas as pl
from jax.experimental.pallas import tpu as pltpu
from jax.sharding import PartitionSpec as P

AXES = ("grp", "dev")
FILL = 512
SLOTS = 8


def whiten(spectra):
    real_part = spectra[:, 0, :].astype(jnp.float32)
    imag_part = spectra[:, 1, :].astype(jnp.float32)
    magnitude = jnp.sqrt(real_part * real_part + imag_part * imag_part)
    factor = 1.0 / jnp.maximum(magnitude, 0.25)
    pair = jnp.concatenate([real_part * factor, imag_part * factor], axis=1)
    return pair.astype(jnp.bfloat16)


def make_table(freqs, lags):
    bins = np.arange(freqs, dtype=np.int64)[None, :]
    shifts = np.arange(lags, dtype=np.int64)[:, None] - lags // 2
    modulus = (bins * shifts) % (2 * freqs)
    angle = modulus.astype(np.float64) * (math.pi / freqs)
    table = np.concatenate([np.cos(angle), -np.sin(angle)], axis=1) / math.sqrt(freqs)
    return jnp.asarray(table.astype(np.float32).astype(ml_dtypes.bfloat16))


def segment_of(channel_ids, seg_lengths):
    bounds = jnp.cumsum(seg_lengths)[:-1]
    return jnp.sum((channel_ids[:, None] >= bounds[None, :]).astype(jnp.int32), axis=1)


def mixing_weights(seg_ids, taps, count):
    width = (taps.shape[0] - 1) // 2
    centre = seg_ids[width : width + count]
    columns = []
    for offset in range(taps.shape[0]):
        same = (seg_ids[offset : offset + count] == centre).astype(jnp.float32)
        columns.append(taps[offset] * same)
    return jnp.stack(columns, axis=0)


def weights_kernel(receivers, table, weights):
    count, lags, freqs = receivers.shape[0], table.shape[0], table.shape[1] // 2
    fill = min(FILL, freqs)

    def body(step, _):
        first = pl.multiple_of(step * fill, fill)
        low, high = pl.ds(first, fill), pl.ds(freqs + first, fill)
        cosine = table[:, low].astype(jnp.float32)
        sine = table[:, high].astype(jnp.float32)
        for c in range(count):
            real_part = receivers[pl.ds(c, 1), low].astype(jnp.float32)
            imag_part = receivers[pl.ds(c, 1), high].astype(jnp.float32)
            rows = pl.ds(c * lags, lags)
            weights[rows, low] = (real_part * cosine - imag_part * sine).astype(jnp.bfloat16)
            weights[rows, high] = (imag_part * cosine + real_part * sine).astype(jnp.bfloat16)
        return 0

    lax.fori_loop(0, freqs // fill, body, 0)


def make_weights(receivers, table):
    count, bins = receivers.shape
    lags = table.shape[0]
    return pl.pallas_call(
        weights_kernel,
        out_shape=pltpu.VMEM((count * lags, bins), jnp.bfloat16),
        in_specs=[pl.BlockSpec(memory_space=pltpu.VMEM)] * 2,
        out_specs=pl.BlockSpec(memory_space=pltpu.VMEM),
        compiler_params=pltpu.CompilerParams(vmem_limit_bytes=8 << 20),
        cost_estimate=pl.CostEstimate(
            flops=3 * count * lags * bins, bytes_accessed=2 * count * lags * bins, transcendentals=0
        ),
        name="make_weights",
    )(receivers, table)


def edge_weights_kernel(first, high, low, table, weights, white):
    lags, freqs = table.shape[0], table.shape[1] // 2
    lanes = high.shape[1]
    half = freqs // lanes
    count = (high.shape[0] - first) // (2 * half)
    for side, edges in enumerate((high, low)):
        for c in range(count):
            at = first + c * 2 * half
            real_part = edges[pl.ds(at, half), :].astype(jnp.float32)
            imag_part = edges[pl.ds(at + half, half), :].astype(jnp.float32)
            magnitude = jnp.sqrt(real_part * real_part + imag_part * imag_part)
            factor = 1.0 / jnp.maximum(magnitude, 0.25)
            to = (side * count + c) * 2 * half
            for part, row in ((real_part, to), (imag_part, to + half)):
                rounded = (part * factor).astype(jnp.bfloat16)
                white[pl.ds(row, half), :] = rounded.astype(jnp.float32)

    def body(step, _):
        at = pl.multiple_of(step * lanes, lanes)
        low_bins, high_bins = pl.ds(at, lanes), pl.ds(freqs + at, lanes)
        cosine = table[:, low_bins].astype(jnp.float32)
        sine = table[:, high_bins].astype(jnp.float32)
        for c in range(2 * count):
            real_part = white[pl.ds(c * 2 * half + step, 1), :]
            imag_part = white[pl.ds(c * 2 * half + half + step, 1), :]
            rows = pl.ds(c * lags, lags)
            weights[rows, low_bins] = (real_part * cosine - imag_part * sine).astype(jnp.bfloat16)
            weights[rows, high_bins] = (imag_part * cosine + real_part * sine).astype(jnp.bfloat16)
        return 0

    lax.fori_loop(0, half, body, 0)


def make_edge_weights(high, low, first, count, table):
    lags, bins = table.shape
    return pl.pallas_call(
        functools.partial(edge_weights_kernel, first),
        out_shape=pltpu.VMEM((2 * count * lags, bins), jnp.bfloat16),
        in_specs=[pl.BlockSpec(memory_space=pltpu.VMEM)] * 3,
        out_specs=pl.BlockSpec(memory_space=pltpu.VMEM),
        scratch_shapes=[pltpu.VMEM((2 * (high.shape[0] - first), high.shape[1]), jnp.float32)],
        compiler_params=pltpu.CompilerParams(vmem_limit_bytes=8 << 20),
        cost_estimate=pl.CostEstimate(
            flops=6 * count * lags * bins, bytes_accessed=4 * count * lags * bins, transcendentals=0
        ),
        name="make_edge_weights",
    )(high, low, table)


def block_kernel(unit, parts, info, mix, *refs):
    sources = refs[:parts]
    weights_own, weights_edge, kept_own, kept_edge = refs[parts : parts + 4]
    stack_out, filtered_out = refs[-7], refs[-6]
    lhs, corr, stack_buf, filtered_buf, sems = refs[-5:]
    rows = lhs.shape[0]
    units = rows // unit
    steps, _, edges, lags = kept_edge.shape
    taps, shard, _ = mix.shape
    reach = shard + edges
    slots = stack_buf.shape[0]
    width = (taps - 1) // 2
    first = 0
    for part in sources:
        lhs[pl.ds(first, part.shape[0]), :] = part[...]
        first += part.shape[0]
    group = 4
    columns = group * lags

    def product(weights, base):
        def body(step, _):
            at = pl.multiple_of(step * columns, columns)
            out = lax.dot_general(
                lhs[...],
                weights[pl.ds(at, columns), :],
                (((1,), (1,)), ((), ())),
                preferred_element_type=jnp.float32,
            )
            for j in range(group):
                channel = base + step * group + j
                corr[pl.ds(channel, rows, stride=reach), :] = out[:, j * lags : (j + 1) * lags]
            return 0

        lax.fori_loop(0, weights.shape[0] // columns, body, 0)

    product(weights_own, 0)
    product(weights_edge, shard)

    def copies(slot, step, row):
        return (
            pltpu.make_async_copy(
                stack_buf.at[slot], stack_out.at[step, pl.ds(row, unit)], sems.at[0, slot]
            ),
            pltpu.make_async_copy(
                filtered_buf.at[slot], filtered_out.at[step, pl.ds(row, unit)], sems.at[1, slot]
            ),
        )

    def finish(slot):
        for copy in copies(slot, 0, 0):
            copy.wait()

    def visit(number, used):
        u, step = number // steps, number % steps
        row = info[steps + units + u]

        def work(used):
            slot = used % slots

            @pl.when(used >= slots)
            def _():
                finish(slot)

            for i in range(unit):
                at = pl.multiple_of((u * unit + i) * reach, 8)
                near = corr[pl.ds(at, shard), :] + kept_own[step, row + i].astype(jnp.float32)
                edge = corr[pl.ds(at + shard, edges), :] + kept_edge[step, row + i].astype(jnp.float32)
                whole = jnp.concatenate([near, edge], axis=0)
                stack_buf[slot, i] = near
                total = mix[width] * near
                for offset in range(-width, width + 1):
                    if offset:
                        moved = pltpu.roll(whole, (-offset) % reach, 0)[:shard]
                        total = total + mix[width + offset] * moved
                filtered_buf[slot, i] = total
            for copy in copies(slot, step, row):
                copy.start()
            return used + 1

        return lax.cond(info[step] == info[steps + u], work, lambda used: used, used)

    used = lax.fori_loop(0, units * steps, visit, 0)

    def drain(slot, _):
        @pl.when(slot < used)
        def _():
            finish(slot)

        return 0

    lax.fori_loop(0, slots, drain, 0)


def block(sources, weights, kept, mix, info, unit, outs, out_shape):
    rows = sum(part.shape[0] for part in sources)
    steps, count, edges, lags = kept[1].shape
    taps, shard, _ = mix.shape
    reach = shard + edges
    bins = weights[0].shape[1]
    vmem, anywhere = pl.BlockSpec(memory_space=pltpu.VMEM), pl.BlockSpec(memory_space=pl.ANY)
    carried = list(outs)
    before = 2 + len(sources) + 4
    return pl.pallas_call(
        functools.partial(block_kernel, unit, len(sources)),
        out_shape=(out_shape, out_shape),
        in_specs=[pl.BlockSpec(memory_space=pltpu.SMEM)]
        + [vmem] * (1 + len(sources) + 4)
        + [anywhere] * len(carried),
        out_specs=(anywhere, anywhere),
        scratch_shapes=[
            pltpu.VMEM((rows, bins), jnp.bfloat16),
            pltpu.VMEM((rows * reach, lags), jnp.float32),
            pltpu.VMEM((SLOTS, unit, shard, lags), jnp.float32),
            pltpu.VMEM((SLOTS, unit, shard, lags), jnp.float32),
            pltpu.SemaphoreType.DMA((2, SLOTS)),
        ],
        input_output_aliases={before: 0, before + 1: 1} if carried else {},
        compiler_params=pltpu.CompilerParams(vmem_limit_bytes=12 << 20),
        cost_estimate=pl.CostEstimate(
            flops=2 * rows * bins * reach * lags,
            bytes_accessed=8 * rows * shard * lags,
            transcendentals=0,
        ),
        name="block",
    )(info, mix, *sources, *weights, *kept, *carried)


def pairs(groups, devs, move):
    lines = devs // 4
    listed = []
    for g in range(groups):
        for line in range(lines):
            for side in range(2):
                for core in range(2):
                    h, other, flank, die = move(g, line, side, core)
                    listed.append(
                        (
                            g * devs + (line * 2 + side) * 2 + core,
                            h * devs + (other * 2 + flank) * 2 + die,
                        )
                    )
    return listed


def routes():
    groups, devs = lax.axis_size("grp"), lax.axis_size("dev")
    lines = devs // 4

    def send(value, move):
        return lax.ppermute(value, AXES, pairs(groups, devs, move))

    def along(value):
        return [
            send(value, lambda h, n, s, c, k=k: (h, (n + k) % lines, s, c)) for k in range(1, lines)
        ]

    def second(value):
        return send(value, lambda h, n, s, c: (h, n, 1 - s, c) if c == 0 else (1 - h, n, s, c))

    def third(value):
        return send(value, lambda h, n, s, c: (h, n, 1 - s, c) if c == 1 else (1 - h, n, s, c))

    def across(value):
        return send(value, lambda h, n, s, c: (h, n, s, 1 - c))

    return along, second, third, across


def owners(core, far):
    devs = lax.axis_size("dev")
    lines = devs // 4
    g, d = lax.axis_index("grp"), lax.axis_index("dev")
    line, side = d // 4, (d // 2) % 2
    j = jnp.arange(2, dtype=jnp.int32)[:, None]
    k = jnp.arange(lines, dtype=jnp.int32)[None, :]
    flip_side = jnp.where(core == 0, j, far)
    flip_group = jnp.where(core == 0, far, j)
    at_group, at_side = jnp.bitwise_xor(g, flip_group), jnp.bitwise_xor(side, flip_side)
    at_line = (line - k + lines) % lines
    return (at_group * devs + (at_line * 2 + at_side) * 2 + core).reshape(-1)


def shards(spectra, stack_in, plan, seg_lengths, taps):
    shard, _, freqs = spectra.shape
    steps, source_count, _, lags = stack_in.shape
    width = (taps.shape[0] - 1) // 2
    groups, devs = lax.axis_size("grp"), lax.axis_size("dev")
    total = groups * devs
    group_channels = devs * shard
    reach = shard + 2 * width
    everything = groups == 2 and devs % 4 == 0 and total * shard == 2 * source_count
    table = make_table(freqs, lags)

    own = whiten(spectra)
    along, second, third, across = routes()
    if everything:
        held = along(own)

    edge = steps * source_count * width

    def packed(first):
        stacks = lax.slice_in_dim(stack_in, first, first + width, axis=2)
        raw = lax.slice_in_dim(spectra, first, first + width, axis=0)
        return jnp.concatenate([stacks.reshape(edge, lags), raw.reshape(-1, lags)], axis=0)

    low = lax.ppermute(packed(shard - width), AXES, [(i, i + 1) for i in range(total - 1)])
    high = lax.ppermute(packed(0), AXES, [(i + 1, i) for i in range(total - 1)])

    def stacks_of(edges):
        return edges[:edge].reshape(steps, source_count, width, lags)

    start_channel = lax.axis_index(AXES) * shard
    channel_ids = start_channel + jnp.arange(reach, dtype=jnp.int32) - width
    mixing = mixing_weights(segment_of(channel_ids, seg_lengths), taps, shard)
    mix = jnp.broadcast_to(mixing[:, :, None], mixing.shape + (lags,))

    weights_own = make_weights(own, table)
    if everything:
        held, weights_own, mix = lax.optimization_barrier((held, weights_own, mix))
        first = jnp.concatenate([own] + held, axis=0)
        passed = second(first)
    kept_edge = jnp.concatenate([stacks_of(high), stacks_of(low)], axis=2)
    weights_edge = make_edge_weights(high, low, edge, width, table)
    weights, kept = (weights_own, weights_edge), (stack_in, kept_edge)

    out_shape = jax.ShapeDtypeStruct((steps, source_count, shard, lags), jnp.float32)

    def info_of(plan, channels):
        info = jnp.concatenate([plan, channels // source_count, channels % source_count])
        return info.astype(jnp.int32)

    if everything:
        core = lax.axis_index("dev") % 2
        near_info = info_of(plan, jnp.concatenate([owners(core, 0), owners(1 - core, 0)]) * shard)
        far_info = info_of(plan, jnp.concatenate([owners(core, 1), owners(1 - core, 1)]) * shard)
        passed, weights_edge, kept_edge, near_info, far_info = lax.optimization_barrier(
            (passed, weights_edge, kept_edge, near_info, far_info)
        )
        weights, kept = (weights_own, weights_edge), (stack_in, kept_edge)
        near = jnp.concatenate([first, passed], axis=0)
        far = third(near)
        near_other = across(near)
        outs = block((near, near_other), weights, kept, mix, near_info, shard, (), out_shape)
        far, outs = lax.optimization_barrier((far, outs))
        far_other = across(far)
        return block((far, far_other), weights, kept, mix, far_info, shard, outs, out_shape)
    outs = ()
    for step in range(steps):
        first = plan[step] * source_count
        mine = jnp.where(lax.axis_index("grp") == first // group_channels, own, 0)
        piece = lax.psum(mine.astype(own.dtype), "grp")
        whole = lax.all_gather(piece, "dev", axis=0, tiled=True)
        sources = lax.dynamic_slice_in_dim(whole, first % group_channels, source_count, 0)
        rows = step * source_count + jnp.arange(0, source_count, shard, dtype=jnp.int32)
        info = info_of(jnp.arange(steps, dtype=jnp.int32), rows)
        outs = block((sources,), weights, kept, mix, info, shard, outs, out_shape)
    return outs


def solution(mesh):
    placed = (P(AXES, None, None), P(None, None, AXES, None), P(), P(), P())
    return jax.shard_map(
        shards,
        mesh=mesh,
        in_specs=placed,
        out_specs=(P(None, None, AXES, None), P(None, None, AXES, None)),
        check_vma=False,
    )
```

```python
import functools
import math

import jax
import jax.numpy as jnp
import ml_dtypes
import numpy as np
from jax import lax
from jax.experimental import pallas as pl
from jax.experimental.pallas import tpu as pltpu
from jax.sharding import PartitionSpec as P

AXES = ("grp", "dev")
FILL = 512
SLOTS = 8


def whiten(spectra):
    real_part = spectra[:, 0, :].astype(jnp.float32)
    imag_part = spectra[:, 1, :].astype(jnp.float32)
    magnitude = jnp.sqrt(real_part * real_part + imag_part * imag_part)
    factor = 1.0 / jnp.maximum(magnitude, 0.25)
    pair = jnp.concatenate([real_part * factor, imag_part * factor], axis=1)
    return pair.astype(jnp.bfloat16)


def make_table(freqs, lags):
    bins = np.arange(freqs, dtype=np.int64)[None, :]
    shifts = np.arange(lags, dtype=np.int64)[:, None] - lags // 2
    modulus = (bins * shifts) % (2 * freqs)
    angle = modulus.astype(np.float64) * (math.pi / freqs)
    table = np.concatenate([np.cos(angle), -np.sin(angle)], axis=1) / math.sqrt(freqs)
    return jnp.asarray(table.astype(np.float32).astype(ml_dtypes.bfloat16))


VMEM = pl.BlockSpec(memory_space=pltpu.VMEM)
SMEM = pl.BlockSpec(memory_space=pltpu.SMEM)
ANY = pl.BlockSpec(memory_space=pl.ANY)


def mix_weights(seg_lengths, taps, mix):
    count, shard, lags = mix.shape
    width = (count - 1) // 2
    start = (lax.axis_index("grp") * lax.axis_size("dev") + lax.axis_index("dev")) * shard
    ids = start + lax.broadcasted_iota(jnp.int32, (shard, lags), 0)
    segs = [jnp.zeros((shard, lags), jnp.int32) for _ in range(count)]
    bound = 0
    for m in range(seg_lengths.shape[0] - 1):
        bound = bound + seg_lengths[m]
        for offset in range(count):
            segs[offset] += jnp.where(ids >= bound - (offset - width), 1, 0)
    for offset in range(count):
        mix[offset] = jnp.where(segs[offset] == segs[width], taps[offset], 0.0)


def weights_kernel(receivers, table, weights):
    count, lags, freqs = receivers.shape[0], table.shape[0], table.shape[1] // 2
    fill = min(FILL, freqs)

    def body(step, _):
        first = pl.multiple_of(step * fill, fill)
        low, high = pl.ds(first, fill), pl.ds(freqs + first, fill)
        cosine = table[:, low].astype(jnp.float32)
        sine = table[:, high].astype(jnp.float32)
        for c in range(count):
            real_part = receivers[pl.ds(c, 1), low].astype(jnp.float32)
            imag_part = receivers[pl.ds(c, 1), high].astype(jnp.float32)
            rows = pl.ds(c * lags, lags)
            weights[rows, low] = (real_part * cosine - imag_part * sine).astype(jnp.bfloat16)
            weights[rows, high] = (imag_part * cosine + real_part * sine).astype(jnp.bfloat16)
        return 0

    lax.fori_loop(0, freqs // fill, body, 0)


def make_weights(receivers, table):
    count, bins = receivers.shape
    lags = table.shape[0]
    return pl.pallas_call(
        weights_kernel,
        out_shape=pltpu.VMEM((count * lags, bins), jnp.bfloat16),
        in_specs=[VMEM, VMEM],
        out_specs=VMEM,
        compiler_params=pltpu.CompilerParams(vmem_limit_bytes=8 << 20),
        cost_estimate=pl.CostEstimate(
            flops=3 * count * lags * bins, bytes_accessed=2 * count * lags * bins, transcendentals=0
        ),
        name="make_weights",
    )(receivers, table)


def pack_kernel(width, own, stack_in, to_next, to_last, spread, rows):
    steps, sources, shard, lags = stack_in.shape
    unit = spread.shape[0] // shard
    groups = sources // unit
    sides = ((to_next, shard - width), (to_last, 0))

    def body(number, _):
        step, at = number // groups, pl.multiple_of(number % groups * unit, unit)
        spread[...] = stack_in[step, pl.ds(at, unit)].astype(jnp.float32).reshape(unit * shard, lags)
        for to, first in sides:
            for c in range(width):
                part = spread[pl.ds(first + c, unit, stride=shard), :]
                row = pl.multiple_of((step * width + c) * sources + at, unit)
                to[pl.ds(row, unit), :] = part.astype(jnp.bfloat16)
        return 0

    lax.fori_loop(0, steps * groups, body, 0)
    pieces = own.shape[1] // lags
    for to, first in sides:
        for j in range(pieces):
            part = own[:, j * lags : (j + 1) * lags].astype(jnp.float32)
            rows[pl.ds(j * width, width), :] = part[first : first + width]
        to[pl.ds(steps * width * sources, pieces * width), :] = rows[...].astype(jnp.bfloat16)


def pack(own, stack_in, width):
    steps, sources, shard, lags = stack_in.shape
    pieces = own.shape[1] // lags
    shape = jax.ShapeDtypeStruct((width * (steps * sources + pieces), lags), jnp.bfloat16)
    return pl.pallas_call(
        functools.partial(pack_kernel, width),
        out_shape=(shape, shape),
        in_specs=[VMEM, VMEM],
        out_specs=(VMEM, VMEM),
        scratch_shapes=[
            pltpu.VMEM((16 * shard, lags), jnp.float32),
            pltpu.VMEM((pieces * width, lags), jnp.float32),
        ],
        compiler_params=pltpu.CompilerParams(vmem_limit_bytes=8 << 20),
        cost_estimate=pl.CostEstimate(
            flops=0, bytes_accessed=2 * stack_in.size, transcendentals=0
        ),
        name="pack",
    )(own, stack_in)


def join_kernel(*refs):
    parts, out, sems = refs[:-2], refs[-2], refs[-1]
    copies, at = [], 0
    for number, part in enumerate(parts):
        to = out.at[pl.ds(at, part.shape[0])]
        copies.append(pltpu.make_async_copy(part, to, sems.at[number]))
        at += part.shape[0]
    for copy in copies:
        copy.start()
    for copy in copies:
        copy.wait()


def join(parts):
    rows = sum(part.shape[0] for part in parts)
    return pl.pallas_call(
        join_kernel,
        out_shape=pltpu.VMEM((rows, parts[0].shape[1]), parts[0].dtype),
        in_specs=[ANY] * len(parts),
        out_specs=VMEM,
        scratch_shapes=[pltpu.SemaphoreType.DMA((len(parts),))],
        compiler_params=pltpu.CompilerParams(vmem_limit_bytes=2 << 20),
        cost_estimate=pl.CostEstimate(
            flops=0, bytes_accessed=2 * rows * parts[0].shape[1], transcendentals=0
        ),
        name="join",
    )(*parts)


def edge_weights_kernel(first, high, low, table, weights, white):
    lags, freqs = table.shape[0], table.shape[1] // 2
    lanes = high.shape[1]
    pieces = 2 * freqs // lanes
    count = (high.shape[0] - first) // pieces
    size = pieces * count
    for side, edges in enumerate((high, low)):
        white[pl.ds(side * size, size), :] = edges[pl.ds(first, size), :].astype(jnp.float32)

    def body(step, _):
        at = pl.multiple_of(step * lanes, lanes)
        low_bins, high_bins = pl.ds(at, lanes), pl.ds(freqs + at, lanes)
        cosine = table[:, low_bins].astype(jnp.float32)
        sine = table[:, high_bins].astype(jnp.float32)
        for c in range(2 * count):
            row = c // count * size + step * count + c % count
            real_part = white[pl.ds(row, 1), :]
            imag_part = white[pl.ds(row + size // 2, 1), :]
            rows = pl.ds(c * lags, lags)
            weights[rows, low_bins] = (real_part * cosine - imag_part * sine).astype(jnp.bfloat16)
            weights[rows, high_bins] = (imag_part * cosine + real_part * sine).astype(jnp.bfloat16)
        return 0

    lax.fori_loop(0, pieces // 2, body, 0)


def make_edge_weights(high, low, first, count, table):
    lags, bins = table.shape
    return pl.pallas_call(
        functools.partial(edge_weights_kernel, first),
        out_shape=pltpu.VMEM((2 * count * lags, bins), jnp.bfloat16),
        in_specs=[VMEM] * 3,
        out_specs=VMEM,
        scratch_shapes=[pltpu.VMEM((2 * (high.shape[0] - first), high.shape[1]), jnp.float32)],
        compiler_params=pltpu.CompilerParams(vmem_limit_bytes=8 << 20),
        cost_estimate=pl.CostEstimate(
            flops=6 * count * lags * bins, bytes_accessed=4 * count * lags * bins, transcendentals=0
        ),
        name="make_edge_weights",
    )(high, low, table)


def block_kernel(unit, parts, locate, plan, seg_lengths, taps, *refs):
    sources = refs[:parts]
    weights_own, weights_edge, kept_own, high, low = refs[parts : parts + 5]
    stack_out, filtered_out = refs[-9], refs[-8]
    lhs, corr, mix, edge_buf, stack_buf, filtered_buf, sems = refs[-7:]
    rows = lhs.shape[0]
    units = rows // unit
    steps, count, shard, lags = kept_own.shape
    width = (taps.shape[0] - 1) // 2
    edges = 2 * width
    reach = shard + edges
    slots = stack_buf.shape[0]
    mix_weights(seg_lengths, taps, mix)
    first = 0
    for part in sources:
        lhs[pl.ds(first, part.shape[0]), :] = part[...]
        first += part.shape[0]
    group = 4
    columns = group * lags

    def product(weights, base):
        def body(step, _):
            at = pl.multiple_of(step * columns, columns)
            out = lax.dot_general(
                lhs[...],
                weights[pl.ds(at, columns), :],
                (((1,), (1,)), ((), ())),
                preferred_element_type=jnp.float32,
            )
            for j in range(group):
                channel = base + step * group + j
                corr[pl.ds(channel, rows, stride=reach), :] = out[:, j * lags : (j + 1) * lags]
            return 0

        lax.fori_loop(0, weights.shape[0] // columns, body, 0)

    product(weights_own, 0)
    product(weights_edge, shard)

    def copies(slot, step, row):
        return (
            pltpu.make_async_copy(
                stack_buf.at[slot], stack_out.at[step, pl.ds(row, unit)], sems.at[0, slot]
            ),
            pltpu.make_async_copy(
                filtered_buf.at[slot], filtered_out.at[step, pl.ds(row, unit)], sems.at[1, slot]
            ),
        )

    def finish(slot):
        for copy in copies(slot, 0, 0):
            copy.wait()

    def visit(number, used):
        u, step = number // steps, number % steps
        wanted, row = locate(u, step, plan)
        row = pl.multiple_of(row, unit)

        def work(used):
            slot = used % slots

            @pl.when(used >= slots)
            def _():
                finish(slot)

            for c in range(width):
                at = pl.multiple_of((step * width + c) * count + row, unit)
                edge_buf[pl.ds(c, unit, stride=edges), :] = high[pl.ds(at, unit), :].astype(jnp.float32)
                edge_buf[pl.ds(width + c, unit, stride=edges), :] = low[pl.ds(at, unit), :].astype(
                    jnp.float32
                )
            for i in range(unit):
                at = pl.multiple_of((u * unit + i) * reach, 8)
                near = corr[pl.ds(at, shard), :] + kept_own[step, row + i].astype(jnp.float32)
                edge = corr[pl.ds(at + shard, edges), :] + edge_buf[pl.ds(i * edges, edges), :]
                whole = jnp.concatenate([near, edge], axis=0)
                stack_buf[slot, i] = near
                total = mix[width] * near
                for offset in range(-width, width + 1):
                    if offset:
                        moved = pltpu.roll(whole, (-offset) % reach, 0)[:shard]
                        total = total + mix[width + offset] * moved
                filtered_buf[slot, i] = total
            for copy in copies(slot, step, row):
                copy.start()
            return used + 1

        return lax.cond(wanted, work, lambda used: used, used)

    used = lax.fori_loop(0, units * steps, visit, 0)

    def drain(slot, _):
        @pl.when(slot < used)
        def _():
            finish(slot)

        return 0

    lax.fori_loop(0, slots, drain, 0)


def block(sources, weights, kept, small, locate, outs, out_shape):
    rows = sum(part.shape[0] for part in sources)
    steps, count, shard, lags = kept[0].shape
    taps = small[2].shape[0]
    edges = taps - 1
    reach = shard + edges
    bins = weights[0].shape[1]
    carried = list(outs)
    before = 3 + len(sources) + 5
    return pl.pallas_call(
        functools.partial(block_kernel, shard, len(sources), locate),
        out_shape=(out_shape, out_shape),
        in_specs=[SMEM] * 3 + [VMEM] * (len(sources) + 5) + [ANY] * len(carried),
        out_specs=(ANY, ANY),
        scratch_shapes=[
            pltpu.VMEM((rows, bins), jnp.bfloat16),
            pltpu.VMEM((rows * reach, lags), jnp.float32),
            pltpu.VMEM((taps, shard, lags), jnp.float32),
            pltpu.VMEM((shard * edges, lags), jnp.float32),
            pltpu.VMEM((SLOTS, shard, shard, lags), jnp.float32),
            pltpu.VMEM((SLOTS, shard, shard, lags), jnp.float32),
            pltpu.SemaphoreType.DMA((2, SLOTS)),
        ],
        input_output_aliases={before: 0, before + 1: 1} if carried else {},
        compiler_params=pltpu.CompilerParams(vmem_limit_bytes=12 << 20),
        cost_estimate=pl.CostEstimate(
            flops=2 * rows * bins * reach * lags,
            bytes_accessed=8 * rows * shard * lags,
            transcendentals=0,
        ),
        name="block",
    )(*small, *sources, *weights, *kept, *carried)


def pairs(groups, devs, move):
    lines = devs // 4
    listed = []
    for g in range(groups):
        for line in range(lines):
            for side in range(2):
                for core in range(2):
                    h, other, flank, die = move(g, line, side, core)
                    listed.append(
                        (
                            g * devs + (line * 2 + side) * 2 + core,
                            h * devs + (other * 2 + flank) * 2 + die,
                        )
                    )
    return listed


def routes():
    groups, devs = lax.axis_size("grp"), lax.axis_size("dev")
    lines = devs // 4

    def send(value, move):
        return lax.ppermute(value, AXES, pairs(groups, devs, move))

    def along(value):
        return [
            send(value, lambda h, n, s, c, k=k: (h, (n + k) % lines, s, c)) for k in range(1, lines)
        ]

    def second(value):
        return send(value, lambda h, n, s, c: (h, n, 1 - s, c) if c == 0 else (1 - h, n, s, c))

    def third(value):
        return send(value, lambda h, n, s, c: (h, n, 1 - s, c) if c == 1 else (1 - h, n, s, c))

    def across(value):
        return send(value, lambda h, n, s, c: (h, n, s, 1 - c))

    return along, second, third, across


def locate_held(far, shard, source_count, u, step, plan):
    devs = lax.axis_size("dev")
    lines = devs // 4
    g, d = lax.axis_index("grp"), lax.axis_index("dev")
    line, side, core = d // 4, (d // 2) % 2, d % 2
    held, within = u // (2 * lines), u % (2 * lines)
    die = jnp.bitwise_xor(core, held)
    j, k = within // lines, within % lines
    at_side = jnp.bitwise_xor(side, jnp.where(die == 0, j, far))
    at_group = jnp.bitwise_xor(g, jnp.where(die == 0, far, j))
    at_line = (line - k + lines) % lines
    channel = (at_group * devs + (at_line * 2 + at_side) * 2 + die) * shard
    return channel // source_count == plan[step], channel % source_count


def locate_step(this, shard, u, step, plan):
    return step == this, u * shard


def shards(spectra, stack_in, plan, seg_lengths, taps):
    shard, _, freqs = spectra.shape
    steps, source_count, _, lags = stack_in.shape
    width = (taps.shape[0] - 1) // 2
    groups, devs = lax.axis_size("grp"), lax.axis_size("dev")
    total = groups * devs
    group_channels = devs * shard
    everything = groups == 2 and devs % 4 == 0 and total * shard == 2 * source_count
    table = make_table(freqs, lags)

    own = whiten(spectra)
    along, second, third, across = routes()
    if everything:
        held = along(own)

    to_next, to_last = pack(own, stack_in, width)
    low = lax.ppermute(to_next, AXES, [(i, i + 1) for i in range(total - 1)])
    high = lax.ppermute(to_last, AXES, [(i + 1, i) for i in range(total - 1)])
    weights_own = make_weights(own, table)
    small = (plan, seg_lengths, taps)
    if everything:
        held, weights_own = lax.optimization_barrier((held, weights_own))
        first = join([own] + held)
        passed = second(first)
    weights_edge = make_edge_weights(high, low, steps * width * source_count, width, table)
    out_shape = jax.ShapeDtypeStruct((steps, source_count, shard, lags), jnp.float32)
    if everything:
        passed, weights_edge = lax.optimization_barrier((passed, weights_edge))
        weights, kept = (weights_own, weights_edge), (stack_in, high, low)
        near = jnp.concatenate([first, passed], axis=0)
        far = third(near)
        near_other = across(near)
        outs = ()
        locate = functools.partial(locate_held, 0, shard, source_count)
        outs = block((near, near_other), weights, kept, small, locate, outs, out_shape)
        far, outs = lax.optimization_barrier((far, outs))
        far_other = across(far)
        locate = functools.partial(locate_held, 1, shard, source_count)
        return block((far, far_other), weights, kept, small, locate, outs, out_shape)
    weights, kept, outs = (weights_own, weights_edge), (stack_in, high, low), ()
    for step in range(steps):
        first = plan[step] * source_count
        mine = jnp.where(lax.axis_index("grp") == first // group_channels, own, 0)
        piece = lax.psum(mine.astype(own.dtype), "grp")
        whole = lax.all_gather(piece, "dev", axis=0, tiled=True)
        sources = lax.dynamic_slice_in_dim(whole, first % group_channels, source_count, 0)
        locate = functools.partial(locate_step, step, shard)
        outs = block((sources,), weights, kept, small, locate, outs, out_shape)
    return outs


def solution(mesh):
    placed = (P(AXES, None, None), P(None, None, AXES, None), P(), P(), P())
    return jax.shard_map(
        shards,
        mesh=mesh,
        in_specs=placed,
        out_specs=(P(None, None, AXES, None), P(None, None, AXES, None)),
        check_vma=False,
    )
```
